512 devices in a mesh: blk: 256 (over x, y_hi, z, core), tgt: 2 (over y_lo).
Axes of the slice: x: 4, y: 4 (y_hi: 2, y_lo: 2; y = y_hi * 2 + y_lo), z: 16, core: 2. Of those that a mesh axis runs over, the one named last changes fastest.
Arguments:
- gradients: bfloat16 [131072, 8192], P('blk', 'tgt'), may hold values from -6 to 6
- targets: bfloat16 [131072, 64], P('blk'), may hold values from -0.15625 to 0.15625
Outputs:
- kernel_tiles: bfloat16 [3, 131072, 512], P(None, ('blk', 'tgt'))
- influence: float32 [131072, 64], P(('blk', 'tgt'))
The draws below stay inside these ranges and needn't reach their ends.
All inputs are finite; a program needn't handle non-finite values.
Results may differ from the reference program's by a relative error of at most 0.0029.
Values may be sent and summed in bfloat16 or wider, within the bound.
A program may use at most 64 MiB of HBM per device.

```python
import jax
import jax.numpy as jnp
from jax import lax

P_SIZE = 8192
C = 64
E = 512
ROUNDS = 2
EXAMPLES = 131072
N_BLK = 256


def levels(rng, dims, cuts, least, high):
    factor_of = 1.0
    for axis_at, parts in cuts:
        heights = jax.random.uniform(jax.random.fold_in(jax.random.fold_in(rng, 6), axis_at), (parts,), jnp.float32, least / len(cuts), high / len(cuts))
        factor_of = factor_of * jnp.repeat(jnp.exp(heights), dims[axis_at] // parts).reshape((-1,) + (1,) * (len(dims) - 1 - axis_at))
    return factor_of


def gaussian(key, shape, deviation, reach, split=(), held_as=jnp.bfloat16):
    level = levels(key, shape, split, -0.22, 0.18) if split else 1.0
    array = jax.random.normal(key, shape, jnp.float32) * deviation * level
    return jnp.minimum(jnp.maximum(array, -reach), reach).astype(held_as)


def setup_inputs(seed: int = 0) -> dict:
    keys = jax.random.split(jax.random.key(seed), 3)
    gradients = gaussian(keys[0], (EXAMPLES, P_SIZE), 1.0, 6.0, ((0, 256), (1, 2)))
    targets = gaussian(keys[1], (EXAMPLES, C), (E * (ROUNDS + 1)) ** -0.5, 0.15625, ((0, 256),))
    return dict(gradients=gradients, targets=targets)


def reference(gradients, targets):
    scale = 1.0 / (P_SIZE ** 0.5)
    grads_blocks = gradients.reshape(N_BLK, E, P_SIZE)
    targ_blocks = targets.reshape(N_BLK, E, C)

    def self_work(index):
        own = grads_blocks[index]
        kernel = (jnp.dot(own, own.T, preferred_element_type=jnp.float32) * scale).astype(jnp.bfloat16)
        return kernel, jnp.dot(kernel, targ_blocks[index], preferred_element_type=jnp.float32)

    self_tiles, self_out = lax.map(self_work, jnp.arange(N_BLK, dtype=jnp.int32))
    tile_list = [self_tiles.reshape(N_BLK * E, E)]
    influence = self_out.reshape(N_BLK * E, C)
    for level in range(ROUNDS):
        stride = 2 ** level
        groups = N_BLK // (2 * stride)
        grads_five = gradients.reshape(groups, 2, stride, E, P_SIZE)
        targ_five = targets.reshape(groups, 2, stride, E, C)

        def pair_work(index):
            group = index // stride
            member = index % stride
            lower = grads_five[group, 0, member]
            upper = grads_five[group, 1, member]
            kernel = (jnp.dot(lower, upper.T, preferred_element_type=jnp.float32) * scale).astype(jnp.bfloat16)
            low_out = jnp.dot(kernel, targ_five[group, 1, member], preferred_element_type=jnp.float32)
            high_out = jnp.dot(kernel.T, targ_five[group, 0, member], preferred_element_type=jnp.float32)
            return kernel, kernel.T, low_out, high_out

        low_tile, high_tile, low_out, high_out = lax.map(pair_work, jnp.arange(N_BLK // 2, dtype=jnp.int32))
        tiles = jnp.stack([low_tile.reshape(groups, stride, E, E), high_tile.reshape(groups, stride, E, E)], 1)
        tile_list.append(tiles.reshape(N_BLK * E, E))
        outs = jnp.stack([low_out.reshape(groups, stride, E, C), high_out.reshape(groups, stride, E, C)], 1)
        influence = influence + outs.reshape(N_BLK * E, C)
    return jnp.stack(tile_list, 0), influence
```

```python
import functools

import jax
import jax.numpy as jnp
from jax import lax
from jax.experimental import pallas as pl
from jax.experimental.pallas import tpu as pltpu
from jax.sharding import PartitionSpec as P

MESH = pl.DeviceIdType.MESH
NT = (((1,), (1,)), ((), ()))
HALF_GROUPS = ((0, 128), (128, 64), (192, 64))
LAST_PIECES = 4
STEP = 1024


def chunk_list(half, features):
    groups = [(h * half + start, rows) for h in range(2) for start, rows in HALF_GROUPS]
    chunks = []
    for index, (start, rows) in enumerate(groups):
        pieces = LAST_PIECES if index == len(groups) - 1 else 1
        width = features // pieces
        chunks.append([(start, rows, at * width, width) for at in range(pieces)])
    return groups, chunks


def kernel(
    scale,
    grads_hbm, targ_hbm, tiles_hbm, infl_hbm,
    own, other, targ, packed, packed_in, self_out, self_in, self_keep, self_tile,
    part_out, part_in, part_keep, staged, mine, result, infl,
    own_sem, targ_sem, grad_send, grad_recv, pack_send, pack_recv, self_send, self_recv,
    part_send, part_recv, res_send, res_recv, out_sem,
):
    rows, features = grads_hbm.shape
    half = rows // 2
    blk, y = lax.axis_index("blk"), lax.axis_index("tgt")
    core, z = lax.rem(blk, 2), lax.rem(blk // 2, 2)
    chip_blk, z_blk = blk + 1 - 2 * core, blk + 2 - 4 * z
    role = lax.rem(core + z, 2)
    sink = chip_blk + role * (z_blk - chip_blk)
    src = z_blk + role * (chip_blk - z_blk)
    slot_made, slot_got = 2 - role, 1 + role
    y_other = 1 - y
    groups, chunks = chunk_list(half, features)
    per_half = len(HALF_GROUPS)

    def there(block, side):
        return {"blk": block, "tgt": side}

    def half_rows(side):
        return pl.ds(pl.multiple_of(side * half, half), half)

    load_own = pltpu.make_async_copy(grads_hbm, own, own_sem)
    load_own.start()
    load_targ = pltpu.make_async_copy(targ_hbm, targ, targ_sem)
    load_targ.start()

    barrier = pltpu.get_barrier_semaphore()
    for peer in (there(chip_blk, y), there(z_blk, y), there(blk, y_other), there(z_blk, y_other), there(chip_blk, y_other)):
        pl.semaphore_signal(barrier, inc=1, device_id=peer, device_id_type=MESH)
    pl.semaphore_wait(barrier, 5)

    def remote(source, target, send, recv, device):
        return pltpu.make_async_remote_copy(
            src_ref=source, dst_ref=target, send_sem=send, recv_sem=recv, device_id=device, device_id_type=MESH
        )

    grad_copies = []
    for pieces in chunks:
        for start, count, first, width in pieces:
            at = len(grad_copies)
            where = (pl.ds(start, count), pl.ds(first, width))
            copy = remote(grads_hbm.at[where], other.at[where], grad_send.at[at], grad_recv.at[at], there(sink, y))
            copy.start()
            grad_copies.append(copy)

    def contract(left, left_rows, right_rows, first, width, init):
        def body(k, total):
            cols = pl.ds(pl.multiple_of(first + k * STEP, STEP), STEP)
            return total + lax.dot_general(
                left[left_rows, cols], own[right_rows, cols], NT, preferred_element_type=jnp.float32
            )

        return lax.fori_loop(0, width // STEP, body, init)

    load_own.wait()
    zero = jnp.zeros((128, half), jnp.float32)
    for into, side in ((self_out, y_other), (self_keep, y)):
        for r in range(half // 128):
            left_rows = pl.ds(pl.multiple_of(side * half + r * 128, 128), 128)
            for n in range(2):
                into[pl.ds(r * 128, 128), pl.ds(n * half, half)] = contract(
                    own, left_rows, pl.ds(n * half, half), 0, features, zero
                )
        if into is self_out:
            self_copy = remote(self_out, self_in, self_send, self_recv, there(blk, y_other))
            self_copy.start()

    load_targ.wait()
    packed[:, : targ.shape[1]] = targ[pl.ds(0, half), :]
    packed[:, targ.shape[1] :] = targ[pl.ds(half, half), :]

    part_copies = [
        remote(
            part_out.at[pl.ds(start, count)], part_in.at[pl.ds(start, count)],
            part_send.at[g], part_recv.at[g], there(blk, y_other),
        )
        for g, (start, count) in enumerate(groups)
    ]
    res_copies = [
        remote(
            staged.at[pl.ds(start, count)], result.at[y, pl.ds(start % half, count)],
            res_send.at[g], res_recv.at[y, g % per_half], there(src, g // per_half),
        )
        for g, (start, count) in enumerate(groups)
    ]

    def finish(g):
        start, count = groups[g]
        part_copies[g].wait_recv()
        here = pl.ds(start, count)
        staged[here, :] = ((part_keep[here, :] + part_in[here, :]) * scale).astype(jnp.bfloat16)

    def turn(g):
        end = groups[g][0] + groups[g][1]
        if end % 128 == 0:
            here = pl.ds(end - 128, 128)
            block = (part_keep[here, :] + part_in[here, :]) * scale
            mine[:, end - 128 : end] = block.T.astype(jnp.bfloat16)

    at = 0
    for g, (start, count) in enumerate(groups):
        here = pl.ds(start, count)
        for piece, (_, _, first, width) in enumerate(chunks[g]):
            grad_copies[at].wait_recv()
            at += 1
            zeros = jnp.zeros((count, half), jnp.float32)
            last = piece == len(chunks[g]) - 1
            for into, side in ((part_out, y_other), (part_keep, y)):
                into[here, :] = contract(
                    other, here, half_rows(side), first, width, zeros if piece == 0 else into[here, :]
                )
                if last and into is part_out:
                    part_copies[g].start()
        if g >= 1:
            finish(g - 1)
            turn(g - 1)
        if g == 0:
            self_copy.wait_recv()
            self_tile[...] = ((self_keep[...] + self_in[...]) * scale).astype(jnp.bfloat16)
            put_self = pltpu.make_async_copy(self_tile, tiles_hbm.at[0], out_sem.at[0])
            put_self.start()

    for copy in res_copies[:-1]:
        copy.start()
    pack_copies = [
        remote(packed, packed_in.at[1], pack_send.at[0], pack_recv.at[1], there(src, y)),
        remote(packed, packed_in.at[0], pack_send.at[1], pack_recv.at[0], there(sink, y)),
    ]
    for copy in pack_copies:
        copy.start()

    finish(len(groups) - 1)
    res_copies[-1].start()

    turn(len(groups) - 1)
    put_mine = pltpu.make_async_copy(mine, tiles_hbm.at[slot_made], out_sem.at[1])
    put_mine.start()

    def influence_of(left, right, weights):
        width = weights.shape[1] // 2
        return (
            jnp.dot(left, weights, preferred_element_type=jnp.float32)[:, :width]
            + jnp.dot(right, weights, preferred_element_type=jnp.float32)[:, width:]
        )

    total = influence_of(self_tile[:, :half], self_tile[:, half:], packed[...])
    for copy in pack_copies:
        copy.wait_recv()
    total = total + influence_of(mine[:, :half], mine[:, half:], packed_in[0])
    for side in range(2):
        for k, (start, count) in enumerate(HALF_GROUPS):
            landed = result.at[side, pl.ds(start, count)]
            remote(staged.at[pl.ds(start, count)], landed, res_send.at[k], res_recv.at[side, k], there(sink, y)).wait_recv()
    puts = [
        pltpu.make_async_copy(
            result.at[side], tiles_hbm.at[slot_got, :, pl.ds(side * half, half)], out_sem.at[2 + side]
        )
        for side in range(2)
    ]
    for put in puts:
        put.start()
    total = total + influence_of(result[0], result[1], packed_in[1])
    infl[...] = total
    put_infl = pltpu.make_async_copy(infl, infl_hbm, out_sem.at[4])
    put_infl.start()

    for copy in grad_copies + part_copies + res_copies + pack_copies + [self_copy]:
        copy.wait_send()
    for put in [put_self, put_mine, put_infl] + puts:
        put.wait()


def per_device(gradients, targets):
    rows, features = gradients.shape
    half, columns = rows // 2, targets.shape[1]
    groups, chunks = chunk_list(half, features)
    count = sum(len(pieces) for pieces in chunks)
    bf16, f32 = jnp.bfloat16, jnp.float32
    dma = pltpu.SemaphoreType.DMA
    return pl.pallas_call(
        functools.partial(kernel, 1.0 / (2 * features) ** 0.5),
        out_shape=(
            jax.ShapeDtypeStruct((3, half, rows), bf16),
            jax.ShapeDtypeStruct((half, columns), f32),
        ),
        in_specs=[pl.BlockSpec(memory_space=pl.ANY)] * 2,
        out_specs=[pl.BlockSpec(memory_space=pl.ANY)] * 2,
        scratch_shapes=[
            pltpu.VMEM((rows, features), bf16),
            pltpu.VMEM((rows, features), bf16),
            pltpu.VMEM((rows, columns), bf16),
            pltpu.VMEM((half, 2 * columns), bf16),
            pltpu.VMEM((2, half, 2 * columns), bf16),
            pltpu.VMEM((half, rows), f32),
            pltpu.VMEM((half, rows), f32),
            pltpu.VMEM((half, rows), f32),
            pltpu.VMEM((half, rows), bf16),
            pltpu.VMEM((rows, half), f32),
            pltpu.VMEM((rows, half), f32),
            pltpu.VMEM((rows, half), f32),
            pltpu.VMEM((rows, half), bf16),
            pltpu.VMEM((half, rows), bf16),
            pltpu.VMEM((2, half, half), bf16),
            pltpu.VMEM((half, columns), f32),
            dma, dma, dma((count,)), dma((count,)), dma((2,)), dma((2,)), dma, dma,
            dma((len(groups),)), dma((len(groups),)), dma((len(groups),)), dma((2, len(HALF_GROUPS))), dma((5,)),
        ],
        compiler_params=pltpu.CompilerParams(collective_id=0, has_side_effects=True),
    )(gradients, targets)


def solution(mesh):
    placed = (P("blk", "tgt"), P("blk", None))
    return jax.shard_map(
        per_device,
        mesh=mesh,
        in_specs=placed,
        out_specs=(P(None, ("blk", "tgt"), None), P(("blk", "tgt"), None)),
        check_vma=False,
    )
```

```python
import functools

import jax
import jax.numpy as jnp
from jax import lax
from jax.experimental import pallas as pl
from jax.experimental.pallas import tpu as pltpu
from jax.sharding import PartitionSpec as P

MESH = pl.DeviceIdType.MESH
NT = (((1,), (1,)), ((), ()))
HALF_GROUPS = ((0, 128), (128, 64), (192, 64))
LAST_PIECES = 4
STEP = 1024
TURN = 128


def chunk_list(half, features):
    groups = [(h * half + start, rows) for h in range(2) for start, rows in HALF_GROUPS]
    chunks = []
    for index, (start, rows) in enumerate(groups):
        pieces = LAST_PIECES if index == len(groups) - 1 else 1
        width = features // pieces
        chunks.append([(start, rows, at * width, width) for at in range(pieces)])
    return groups, chunks


def kernel(
    scale,
    grads_hbm, targ_hbm, tiles, infl,
    right, left, targ_own, targ_chip, targ_far, targ_pass, self_out, self_in, self_keep,
    part_out, part_in, part_keep, staged, turned,
    in_sem, diag_sem, own_sem, targ_sem, left_send, chip_send, left_recv, right_recv,
    targ_send, targ_recv, self_send, self_recv, part_send, part_recv, res_send, res_recv, turn_send, turn_recv,
):
    rows, features = grads_hbm.shape
    half = rows // 2
    blk, y = lax.axis_index("blk"), lax.axis_index("tgt")
    core, z = lax.rem(blk, 2), lax.rem(blk // 2, 2)
    role = lax.rem(core + z, 2)
    lead, other_role = role == 1, role == 0
    chip = blk + 1 - 2 * core
    far = chip + 2 - 4 * z
    whose = chip + role * (far - chip)
    y_other = 1 - y
    groups, chunks = chunk_list(half, features)
    per_half = len(HALF_GROUPS)
    flat = [piece for pieces in chunks for piece in pieces]

    def there(block, side):
        return {"blk": block, "tgt": side}

    def half_of(side):
        return pl.ds(pl.multiple_of(side * half, half), half)

    def remote(source, target, send, recv, device):
        return pltpu.make_async_remote_copy(
            src_ref=source, dst_ref=target, send_sem=send, recv_sem=recv, device_id=device, device_id_type=MESH
        )

    def signal(sem, device):
        pl.semaphore_signal(sem, inc=1, device_id=device, device_id_type=MESH)

    load_own = pltpu.make_async_copy(grads_hbm, right.at[0], own_sem)
    load_own.start()
    load_targ = pltpu.make_async_copy(targ_hbm, targ_own, targ_sem)
    load_targ.start()

    barrier = pltpu.get_barrier_semaphore()

    @pl.when(lead)
    def _():
        signal(barrier, there(far, y))
        signal(barrier, there(chip, y))

    signal(barrier, there(blk, y_other))
    pl.semaphore_wait(barrier, 2)

    def left_copy(at, send, block):
        start, count, first, width = flat[at]
        where = (pl.ds(start, count), pl.ds(first, width))
        return remote(grads_hbm.at[where], left.at[where], send.at[at], left_recv.at[at], there(block, y))

    right_copy = remote(grads_hbm, right.at[1], chip_send.at[0], right_recv, there(chip, y))
    targ_to_chip = remote(targ_hbm, targ_chip, targ_send.at[0], targ_recv.at[0], there(chip, y))
    targ_to_far = remote(targ_chip, targ_far, targ_send.at[1], targ_recv.at[1], there(far, y))
    targ_to_pass = remote(targ_hbm, targ_pass, targ_send.at[2], targ_recv.at[2], there(far, y))
    targ_passed = remote(targ_pass, targ_far, targ_send.at[3], targ_recv.at[1], there(chip, y))

    @pl.when(lead)
    def _():
        for at in range(len(flat)):
            left_copy(at, left_send, far).start()
        targ_to_pass.start()

    signal(diag_sem, there(blk, y_other))

    @pl.when(other_role)
    def _():
        signal(in_sem, there(chip, y))
        right_copy.start()
        targ_to_chip.start()

    @pl.when(lead)
    def _():
        pl.semaphore_wait(in_sem, 1)
        for at in range(len(flat)):
            left_copy(at, chip_send, chip).start()
        targ_to_chip.start()

    def contract(lhs, rhs, first, width, init):
        def body(k, total):
            cols = pl.ds(pl.multiple_of(first + k * STEP, STEP), STEP)
            return total + lax.dot_general(lhs(cols), rhs(cols), NT, preferred_element_type=jnp.float32)

        return lax.fori_loop(0, width // STEP, body, init)

    load_own.wait()
    zero = jnp.zeros((128, half), jnp.float32)
    self_copy = remote(self_out, self_in, self_send, self_recv, there(blk, y_other))
    for into, side in ((self_out, y_other), (self_keep, y)):
        for r in range(half // 128):
            mine = pl.ds(pl.multiple_of(side * half + r * 128, 128), 128)
            for n in range(2):
                into[pl.ds(r * 128, 128), pl.ds(n * half, half)] = contract(
                    lambda cols: right[0, mine, cols],
                    lambda cols: right[0, pl.ds(n * half, half), cols],
                    0, features, zero,
                )
        if into is self_out:
            self_copy.start()

    part_copies = [
        remote(
            part_out.at[pl.ds(start, count)], part_in.at[pl.ds(start, count)],
            part_send.at[g], part_recv.at[g], there(blk, y_other),
        )
        for g, (start, count) in enumerate(groups)
    ]

    def res_copy(g, slot, side, block):
        start, count = groups[g]
        return remote(
            staged.at[pl.ds(start, count)],
            tiles.at[slot, pl.ds(start % half, count), half_of(side)],
            res_send.at[g], res_recv.at[slot - 1, side, g % per_half], there(block, g // per_half),
        )

    def turn_copy(n):
        cols = pl.ds(n * TURN, TURN)
        return remote(turned.at[:, cols], tiles.at[2, :, cols], turn_send.at[n], turn_recv.at[n], there(chip, y))

    def finish(g):
        start, count = groups[g]
        part_copies[g].wait_recv()
        here = pl.ds(start, count)
        staged[here, :] = ((part_keep[here, :] + part_in[here, :]) * scale).astype(jnp.bfloat16)
        res_copy(g, 1 + role, y, whose).start()
        end = start + count
        if end % TURN == 0:
            here = pl.ds(end - TURN, TURN)
            block = ((part_keep[here, :] + part_in[here, :]) * scale).T.astype(jnp.bfloat16)

            @pl.when(lead)
            def _():
                turned[:, end - TURN : end] = block
                turn_copy(end // TURN - 1).start()

            @pl.when(other_role)
            def _():
                tiles[1, :, end - TURN : end] = block

    @pl.when(lead)
    def _():
        targ_to_chip.wait_recv()
        targ_to_far.start()
        right_copy.wait_recv()

    pl.semaphore_wait(diag_sem, 1)
    at = 0
    for g, (start, count) in enumerate(groups):
        here = pl.ds(start, count)
        for piece, (_, _, first, width) in enumerate(chunks[g]):
            left_copy(at, left_send, far).wait_recv()
            at += 1
            for into, side in ((part_out, y_other), (part_keep, y)):
                into[here, :] = contract(
                    lambda cols: left[here, cols],
                    lambda cols: right[role, half_of(side), cols],
                    first, width,
                    jnp.zeros((count, half), jnp.float32) if piece == 0 else into[here, :],
                )
                if piece == len(chunks[g]) - 1 and into is part_out:
                    part_copies[g].start()
        if g >= 1:
            finish(g - 1)
        if g == 0:
            self_copy.wait_recv()
            tiles[0] = ((self_keep[...] + self_in[...]) * scale).astype(jnp.bfloat16)
    finish(len(groups) - 1)

    def influence_of(targets, slot):
        return lax.dot_general(targets[...], tiles[slot], NT, preferred_element_type=jnp.float32)

    @pl.when(lead)
    def _():
        targ_to_pass.wait_recv()
        targ_passed.start()
        for side in range(2):
            for g in range(per_half):
                res_copy(g, 1, side, whose).wait_recv()

    @pl.when(other_role)
    def _():
        targ_to_chip.wait_recv()

    load_targ.wait()
    infl[...] = influence_of(targ_own, 0) + influence_of(targ_chip, 1)
    targ_to_far.wait_recv()

    @pl.when(lead)
    def _():
        for side in range(2):
            for g in range(per_half):
                res_copy(g, 2, side, whose).wait_recv()

    @pl.when(other_role)
    def _():
        for n in range(rows // TURN):
            turn_copy(n).wait_recv()

    infl[...] += influence_of(targ_far, 2)

    for g in range(len(groups)):
        part_copies[g].wait_send()
        res_copy(g, 1 + role, y, whose).wait_send()
    self_copy.wait_send()
    targ_to_chip.wait_send()

    @pl.when(lead)
    def _():
        for at in range(len(flat)):
            left_copy(at, left_send, far).wait_send()
            left_copy(at, chip_send, chip).wait_send()
        for copy in (targ_to_far, targ_to_pass, targ_passed):
            copy.wait_send()
        for n in range(rows // TURN):
            turn_copy(n).wait_send()

    @pl.when(other_role)
    def _():
        right_copy.wait_send()


def put_kernel(tiles, infl, tiles_hbm, infl_hbm, sems):
    puts = [pltpu.make_async_copy(infl, infl_hbm, sems.at[3])]
    puts += [pltpu.make_async_copy(tiles.at[slot], tiles_hbm.at[slot], sems.at[slot]) for slot in range(3)]
    for put in puts:
        put.start()
    for put in puts:
        put.wait()


def per_device(gradients, targets):
    rows, features = gradients.shape
    half, columns = rows // 2, targets.shape[1]
    groups, chunks = chunk_list(half, features)
    count = sum(len(pieces) for pieces in chunks)
    bf16, f32 = jnp.bfloat16, jnp.float32
    dma, vmem = pltpu.SemaphoreType.DMA, pltpu.VMEM
    shapes = (jax.ShapeDtypeStruct((3, half, rows), bf16), jax.ShapeDtypeStruct((columns, half), f32))
    tiles, infl = pl.pallas_call(
        functools.partial(kernel, 1.0 / (2 * features) ** 0.5),
        out_shape=shapes,
        in_specs=[pl.BlockSpec(memory_space=pltpu.HBM)] * 2,
        out_specs=[pl.BlockSpec(memory_space=vmem)] * 2,
        scratch_shapes=[
            vmem((2, rows, features), bf16),
            vmem((rows, features), bf16),
            *[vmem((columns, rows), bf16)] * 4,
            *[vmem((half, rows), f32)] * 3,
            *[vmem((rows, half), f32)] * 3,
            vmem((rows, half), bf16),
            vmem((half, rows), bf16),
            pltpu.SemaphoreType.REGULAR, pltpu.SemaphoreType.REGULAR,
            dma, dma, dma((count,)), dma((count,)), dma((count,)), dma,
            dma((4,)), dma((3,)), dma, dma,
            dma((len(groups),)), dma((len(groups),)), dma((len(groups),)), dma((2, 2, len(HALF_GROUPS))),
            dma((rows // TURN,)), dma((rows // TURN,)),
        ],
        compiler_params=pltpu.CompilerParams(
            collective_id=0, has_side_effects=True, vmem_limit_bytes=48 * 2**20
        ),
    )(pltpu.with_memory_space_constraint(gradients, pltpu.HBM), pltpu.with_memory_space_constraint(targets.T, pltpu.HBM))
    tiles, infl = pl.pallas_call(
        put_kernel,
        out_shape=shapes,
        in_specs=[pl.BlockSpec(memory_space=vmem)] * 2,
        out_specs=[pl.BlockSpec(memory_space=pltpu.HBM)] * 2,
        scratch_shapes=[dma((4,))],
        compiler_params=pltpu.CompilerParams(vmem_limit_bytes=16 * 2**20),
    )(tiles, infl)
    return tiles, infl.T


def solution(mesh):
    placed = (P("blk", "tgt"), P("blk", None))
    return jax.shard_map(
        per_device,
        mesh=mesh,
        in_specs=placed,
        out_specs=(P(None, ("blk", "tgt"), None), P(("blk", "tgt"), None)),
        check_vma=False,
    )
```

```python
import functools

import jax
import jax.numpy as jnp
from jax import lax
from jax.experimental import pallas as pl
from jax.experimental.pallas import tpu as pltpu
from jax.sharding import PartitionSpec as P

MESH = pl.DeviceIdType.MESH
NT = (((1,), (1,)), ((), ()))
GROUPS = ((0, 128), (128, 128), (256, 128), (384, 96), (480, 32))
LAST_PIECES = 4
STEP = 1024
TURN = 128


def chunk_list(features):
    chunks = []
    for index, (start, rows) in enumerate(GROUPS):
        pieces = LAST_PIECES if index == len(GROUPS) - 1 else 1
        width = features // pieces
        chunks.append([(start, rows, at * width, width) for at in range(pieces)])
    return chunks


def kernel(
    scale,
    grads_hbm, targ_hbm, tiles, infl,
    right, left, targ_own, targ_chip, targ_far, targ_pass, self_out, self_in, self_keep,
    part_out, part_in, part_keep, staged, last_out, last_in, last_staged, turned,
    in_sem, diag_sem, own_sem, targ_sem, left_send, chip_send, left_recv, right_recv,
    targ_send, targ_recv, self_send, self_recv, part_send, part_recv, res_send, res_recv, turn_send, turn_recv,
):
    rows, features = grads_hbm.shape
    half = rows // 2
    blk, y = lax.axis_index("blk"), lax.axis_index("tgt")
    core, z = lax.rem(blk, 2), lax.rem(blk // 2, 2)
    lead, near = core == 1, core == 0
    streams = lax.rem(core + z, 2) == 1
    lends, borrows = core + z == 0, core - z == 1
    odd_near, odd_lead = z - core == 1, z + core == 2
    chip = blk + 1 - 2 * core
    across = blk - core + 2 - 4 * z
    whose = chip + core * (across + z - chip)
    right_at = core * (1 - z)
    made = 1 + core
    y_other = 1 - y
    groups, chunks, final = GROUPS, chunk_list(features), len(GROUPS) - 1
    flat = [piece for pieces in chunks for piece in pieces]

    def there(block, side):
        return {"blk": block, "tgt": side}

    def half_of(side):
        return pl.ds(pl.multiple_of(side * half, half), half)

    def remote(source, target, send, recv, device):
        return pltpu.make_async_remote_copy(
            src_ref=source, dst_ref=target, send_sem=send, recv_sem=recv, device_id=device, device_id_type=MESH
        )

    def signal(sem, device):
        pl.semaphore_signal(sem, inc=1, device_id=device, device_id_type=MESH)

    load_own = pltpu.make_async_copy(grads_hbm, right.at[0], own_sem)
    load_own.start()
    load_targ = pltpu.make_async_copy(targ_hbm, targ_own, targ_sem)
    load_targ.start()

    barrier = pltpu.get_barrier_semaphore()

    signal(barrier, there(blk, y_other))

    @pl.when(jnp.logical_not(lends))
    def _():
        signal(barrier, there(across + 1, y))

    @pl.when(borrows)
    def _():
        signal(barrier, there(across, y))
        signal(barrier, there(chip, y))

    @pl.when(z == 1)
    def _():
        signal(barrier, there(chip, y))

    pl.semaphore_wait(barrier, 3 - (1 - core) * (1 - z))

    def left_copy(at, send, block):
        start, count, first, width = flat[at]
        where = (pl.ds(start, count), pl.ds(first, width))
        return remote(grads_hbm.at[where], left.at[where], send.at[at], left_recv.at[at], there(block, y))

    right_copy = remote(grads_hbm, right.at[1], chip_send.at[0], right_recv, there(chip, y))
    targ_to_chip = remote(targ_hbm, targ_chip, targ_send.at[0], targ_recv.at[0], there(chip, y))
    targ_to_far = remote(targ_hbm, targ_far, targ_send.at[1], targ_recv.at[1], there(across + 1, y))
    targ_lent = remote(targ_chip, targ_far, targ_send.at[2], targ_recv.at[1], there(across, y))
    targ_to_pass = remote(targ_hbm, targ_pass, targ_send.at[2], targ_recv.at[2], there(across + 1, y))
    targ_passed = remote(targ_pass, targ_far, targ_send.at[3], targ_recv.at[1], there(chip, y))

    @pl.when(streams)
    def _():
        for at in range(len(flat)):
            left_copy(at, left_send, across + 1).start()

    @pl.when(borrows)
    def _():
        targ_to_far.start()
        pl.semaphore_wait(in_sem, 1)

    @pl.when(odd_near)
    def _():
        targ_to_pass.start()

    signal(diag_sem, there(blk, y_other))

    @pl.when(lends)
    def _():
        signal(in_sem, there(chip, y))
        right_copy.start()

    @pl.when(lead)
    def _():
        for at in range(len(flat)):
            left_copy(at, chip_send, chip).start()

    targ_to_chip.start()

    def contract(lhs, rhs, first, width, init):
        def body(k, total):
            cols = pl.ds(pl.multiple_of(first + k * STEP, STEP), STEP)
            return total + lax.dot_general(lhs(cols), rhs(cols), NT, preferred_element_type=jnp.float32)

        return lax.fori_loop(0, width // STEP, body, init)

    load_own.wait()
    zero = jnp.zeros((128, half), jnp.float32)
    self_copy = remote(self_out, self_in, self_send, self_recv, there(blk, y_other))
    for into, side in ((self_out, y_other), (self_keep, y)):
        for r in range(half // 128):
            mine = pl.ds(pl.multiple_of(side * half + r * 128, 128), 128)
            for n in range(2):
                into[pl.ds(r * 128, 128), pl.ds(n * half, half)] = contract(
                    lambda cols: right[0, mine, cols],
                    lambda cols: right[0, pl.ds(n * half, half), cols],
                    0, features, zero,
                )
        if into is self_out:
            self_copy.start()

    part_copies = [
        remote(
            part_out.at[pl.ds(start, count)], part_in.at[pl.ds(start, count)],
            part_send.at[g], part_recv.at[g], there(blk, y_other),
        )
        for g, (start, count) in enumerate(groups[:final])
    ]
    part_copies.append(remote(last_out, last_in, part_send.at[final], part_recv.at[final], there(blk, y_other)))

    def res_copy(g, slot, side):
        start, count = groups[g]
        return remote(
            staged.at[pl.ds(start, count)],
            tiles.at[slot, pl.ds(start % half, count), half_of(side)],
            res_send.at[g], res_recv.at[slot - 1, side, g], there(whose, start // half),
        )

    def last_res_copy(slot):
        start, count = groups[final]
        return remote(
            last_staged, tiles.at[slot, pl.ds(start % half, count), :],
            res_send.at[final], res_recv.at[slot - 1, 0, final], there(whose, start // half),
        )

    holds_last = y == groups[final][0] // half

    def wait_results(slot):
        for g, (start, _) in enumerate(groups):
            @pl.when(y == start // half)
            def _():
                if g == final:
                    last_res_copy(slot).wait_recv()
                else:
                    for side in range(2):
                        res_copy(g, slot, side).wait_recv()

    def turn_copy(n):
        cols = pl.ds(n * TURN, TURN)
        return remote(turned.at[:, cols], tiles.at[2, :, cols], turn_send.at[n], turn_recv.at[n], there(chip, y))

    def finish(g):
        start, count = groups[g]
        end = start + count
        here = pl.ds(start, count)
        part_copies[g].wait_recv()
        if g < final:
            summed = (part_keep[here, :] + part_in[here, :]) * scale
            part_keep[here, :] = summed
            staged[here, :] = summed.astype(jnp.bfloat16)

            @pl.when(near)
            def _():
                res_copy(g, made, y).start()
        else:
            @pl.when(holds_last)
            def _():
                last_staged[...] = ((last_out[...] + last_in[...]) * scale).astype(jnp.bfloat16)
                last_res_copy(made).start()

            part_keep[here, :] = (last_out[:, half_of(y)] + last_in[:, half_of(y)]) * scale
        if end % TURN == 0:
            block = part_keep[end - TURN : end, :].T.astype(jnp.bfloat16)

            @pl.when(borrows)
            def _():
                turned[:, end - TURN : end] = block
                turn_copy(end // TURN - 1).start()

            @pl.when(jnp.logical_not(borrows))
            def _():
                tiles[made, :, end - TURN : end] = block

    def influence_of(targets, slot):
        return lax.dot_general(targets[...], tiles[slot], NT, preferred_element_type=jnp.float32)

    def near_influence():
        infl[...] = influence_of(targ_own, 0) + influence_of(targ_chip, 1)

    targ_to_chip.wait_recv()

    @pl.when(borrows)
    def _():
        targ_lent.start()
        right_copy.wait_recv()

    load_targ.wait()
    pl.semaphore_wait(diag_sem, 1)
    at = 0
    for g, (start, count) in enumerate(groups):
        here = pl.ds(start, count)
        if g == final:
            @pl.when(lead)
            def _():
                wait_results(1)
                near_influence()
        for piece, (_, _, first, width) in enumerate(chunks[g]):
            if g == final and piece == 1:
                @pl.when(lead)
                def _():
                    for early in range(final - 1):
                        res_copy(early, made, y).start()

            left_copy(at, left_send, across + 1).wait_recv()
            at += 1
            if g == final:
                for n in range(2):
                    cols = pl.ds(n * half, half)
                    last_out[:, cols] = contract(
                        lambda k: left[here, k],
                        lambda k: right[right_at, cols, k],
                        first, width,
                        jnp.zeros((count, half), jnp.float32) if piece == 0 else last_out[:, cols],
                    )
                if piece == len(chunks[g]) - 1:
                    part_copies[g].start()
                continue
            for into, side in ((part_out, y_other), (part_keep, y)):
                into[here, :] = contract(
                    lambda k: left[here, k],
                    lambda k: right[right_at, half_of(side), k],
                    first, width, jnp.zeros((count, half), jnp.float32),
                )
                if into is part_out:
                    part_copies[g].start()
        if g >= 1:
            finish(g - 1)
        if g == 0:
            self_copy.wait_recv()
            tiles[0] = ((self_keep[...] + self_in[...]) * scale).astype(jnp.bfloat16)

    @pl.when(lead)
    def _():
        res_copy(final - 1, made, y).start()

    @pl.when(odd_lead)
    def _():
        targ_to_far.start()

    @pl.when(borrows)
    def _():
        targ_to_pass.wait_recv()
        targ_passed.start()

    finish(final)

    @pl.when(near)
    def _():
        near_influence()

    targ_to_far.wait_recv()

    @pl.when(streams)
    def _():
        wait_results(2)

    @pl.when(lends)
    def _():
        for n in range(rows // TURN):
            turn_copy(n).wait_recv()

    infl[...] += influence_of(targ_far, 2)

    for g in range(len(groups)):
        part_copies[g].wait_send()
        if g < final:
            res_copy(g, made, y).wait_send()

    @pl.when(holds_last)
    def _():
        last_res_copy(made).wait_send()

    self_copy.wait_send()
    targ_to_chip.wait_send()

    @pl.when(streams)
    def _():
        for at in range(len(flat)):
            left_copy(at, left_send, across + 1).wait_send()

    @pl.when(lead)
    def _():
        for at in range(len(flat)):
            left_copy(at, chip_send, chip).wait_send()
        targ_to_far.wait_send()

    @pl.when(borrows)
    def _():
        targ_lent.wait_send()
        targ_passed.wait_send()
        for n in range(rows // TURN):
            turn_copy(n).wait_send()

    @pl.when(odd_near)
    def _():
        targ_to_pass.wait_send()

    @pl.when(lends)
    def _():
        right_copy.wait_send()


def put_kernel(tiles, infl, tiles_hbm, infl_hbm, sems):
    puts = [pltpu.make_async_copy(infl, infl_hbm, sems.at[3])]
    puts += [pltpu.make_async_copy(tiles.at[slot], tiles_hbm.at[slot], sems.at[slot]) for slot in range(3)]
    for put in puts:
        put.start()
    for put in puts:
        put.wait()


def per_device(gradients, targets):
    rows, features = gradients.shape
    half, columns = rows // 2, targets.shape[1]
    count = sum(len(pieces) for pieces in chunk_list(features))
    last, groups = GROUPS[-1][1], len(GROUPS)
    bf16, f32 = jnp.bfloat16, jnp.float32
    dma, vmem = pltpu.SemaphoreType.DMA, pltpu.VMEM
    shapes = (jax.ShapeDtypeStruct((3, half, rows), bf16), jax.ShapeDtypeStruct((columns, half), f32))
    tiles, infl = pl.pallas_call(
        functools.partial(kernel, 1.0 / (2 * features) ** 0.5),
        out_shape=shapes,
        in_specs=[pl.BlockSpec(memory_space=pltpu.HBM)] * 2,
        out_specs=[pl.BlockSpec(memory_space=vmem)] * 2,
        scratch_shapes=[
            vmem((2, rows, features), bf16),
            vmem((rows, features), bf16),
            *[vmem((columns, rows), bf16)] * 4,
            *[vmem((half, rows), f32)] * 3,
            *[vmem((rows, half), f32)] * 3,
            vmem((rows, half), bf16),
            vmem((last, rows), f32), vmem((last, rows), f32), vmem((last, rows), bf16),
            vmem((half, rows), bf16),
            pltpu.SemaphoreType.REGULAR, pltpu.SemaphoreType.REGULAR,
            dma, dma, dma((count,)), dma((count,)), dma((count,)), dma,
            dma((4,)), dma((3,)), dma, dma,
            dma((groups,)), dma((groups,)), dma((groups,)), dma((2, 2, groups)),
            dma((rows // TURN,)), dma((rows // TURN,)),
        ],
        compiler_params=pltpu.CompilerParams(
            collective_id=0, has_side_effects=True, vmem_limit_bytes=48 * 2**20
        ),
    )(pltpu.with_memory_space_constraint(gradients, pltpu.HBM), pltpu.with_memory_space_constraint(targets.T, pltpu.HBM))
    tiles, infl = pl.pallas_call(
        put_kernel,
        out_shape=shapes,
        in_specs=[pl.BlockSpec(memory_space=vmem)] * 2,
        out_specs=[pl.BlockSpec(memory_space=pltpu.HBM)] * 2,
        scratch_shapes=[dma((4,))],
        compiler_params=pltpu.CompilerParams(vmem_limit_bytes=16 * 2**20),
    )(tiles, infl)
    return tiles, infl.T


def solution(mesh):
    placed = (P("blk", "tgt"), P("blk", None))
    return jax.shard_map(
        per_device,
        mesh=mesh,
        in_specs=placed,
        out_specs=(P(None, ("blk", "tgt"), None), P(("blk", "tgt"), None)),
        check_vma=False,
    )
```

```python
import functools

import jax
import jax.numpy as jnp
from jax import lax
from jax.experimental import pallas as pl
from jax.experimental.pallas import tpu as pltpu
from jax.sharding import PartitionSpec as P

MESH = pl.DeviceIdType.MESH
NT = (((1,), (1,)), ((), ()))
GROUPS = ((0, 128), (128, 128), (256, 128), (384, 96), (480, 32))
LAST_PIECES = 4
STEP = 1024
TURN = 128


def chunk_list(features):
    chunks = []
    for index, (start, rows) in enumerate(GROUPS):
        pieces = LAST_PIECES if index == len(GROUPS) - 1 else 1
        width = features // pieces
        chunks.append([(start, rows, at * width, width) for at in range(pieces)])
    return chunks


def kernel(
    scale,
    grads_hbm, targ_hbm, tiles, infl,
    right, left, targ_own, targ_chip, targ_far, targ_pass, self_out, self_in, self_keep,
    part_out, part_in, part_keep, staged, last_out, last_in, last_staged, turned,
    in_sem, diag_sem, own_sem, targ_sem, left_send, chip_send, left_recv, right_recv,
    targ_send, targ_recv, self_send, self_recv, part_send, part_recv, res_send, res_recv, turn_send, turn_recv,
):
    rows, features = grads_hbm.shape
    half = rows // 2
    blk, y = lax.axis_index("blk"), lax.axis_index("tgt")
    core, z = lax.rem(blk, 2), lax.rem(blk // 2, 2)
    lead, near = core == 1, core == 0
    streams = lax.rem(core + z, 2) == 1
    lends, borrows = core + z == 0, core - z == 1
    odd_near, odd_lead = z - core == 1, z + core == 2
    chip = blk + 1 - 2 * core
    across = blk - core + 2 - 4 * z
    whose = chip + core * (across + z - chip)
    right_at = core * (1 - z)
    made = 1 + core
    y_other = 1 - y
    groups, chunks, final = GROUPS, chunk_list(features), len(GROUPS) - 1
    flat = [piece for pieces in chunks for piece in pieces]

    def there(block, side):
        return {"blk": block, "tgt": side}

    def half_of(side):
        return pl.ds(pl.multiple_of(side * half, half), half)

    def remote(source, target, send, recv, device):
        return pltpu.make_async_remote_copy(
            src_ref=source, dst_ref=target, send_sem=send, recv_sem=recv, device_id=device, device_id_type=MESH
        )

    def signal(sem, device):
        pl.semaphore_signal(sem, inc=1, device_id=device, device_id_type=MESH)

    load_own = pltpu.make_async_copy(grads_hbm, right.at[0], own_sem)
    load_own.start()
    load_targ = pltpu.make_async_copy(targ_hbm, targ_own, targ_sem)
    load_targ.start()

    barrier = pltpu.get_barrier_semaphore()

    signal(barrier, there(blk, y_other))

    @pl.when(jnp.logical_not(lends))
    def _():
        signal(barrier, there(across + 1, y))

    @pl.when(borrows)
    def _():
        signal(barrier, there(across, y))
        signal(barrier, there(chip, y))

    @pl.when(z == 1)
    def _():
        signal(barrier, there(chip, y))

    pl.semaphore_wait(barrier, 3 - (1 - core) * (1 - z))

    def left_copy(at, send, block):
        start, count, first, width = flat[at]
        where = (pl.ds(start, count), pl.ds(first, width))
        return remote(grads_hbm.at[where], left.at[where], send.at[at], left_recv.at[at], there(block, y))

    right_copy = remote(grads_hbm, right.at[1], chip_send.at[0], right_recv, there(chip, y))
    targ_to_chip = remote(targ_hbm, targ_chip, targ_send.at[0], targ_recv.at[0], there(chip, y))
    targ_to_far = remote(targ_hbm, targ_far, targ_send.at[1], targ_recv.at[1], there(across + 1, y))
    targ_lent = remote(targ_chip, targ_far, targ_send.at[2], targ_recv.at[1], there(across, y))
    targ_to_pass = remote(targ_hbm, targ_pass, targ_send.at[2], targ_recv.at[2], there(across + 1, y))
    targ_passed = remote(targ_pass, targ_far, targ_send.at[3], targ_recv.at[1], there(chip, y))

    @pl.when(streams)
    def _():
        for at in range(len(flat)):
            left_copy(at, left_send, across + 1).start()

    @pl.when(borrows)
    def _():
        targ_to_far.start()
        pl.semaphore_wait(in_sem, 1)

    @pl.when(odd_near)
    def _():
        targ_to_pass.start()

    signal(diag_sem, there(blk, y_other))

    @pl.when(lends)
    def _():
        signal(in_sem, there(chip, y))
        right_copy.start()

    @pl.when(lead)
    def _():
        for at in range(len(flat)):
            left_copy(at, chip_send, chip).start()

    targ_to_chip.start()

    def contract(lhs, rhs, first, width, init):
        def body(k, total):
            cols = pl.ds(pl.multiple_of(first + k * STEP, STEP), STEP)
            return total + lax.dot_general(lhs(cols), rhs(cols), NT, preferred_element_type=jnp.float32)

        return lax.fori_loop(0, width // STEP, body, init)

    load_own.wait()
    zero = jnp.zeros((128, half), jnp.float32)
    self_copy = remote(self_out, self_in, self_send, self_recv, there(blk, y_other))
    for into, side in ((self_out, y_other), (self_keep, y)):
        for r in range(half // 128):
            mine = pl.ds(pl.multiple_of(side * half + r * 128, 128), 128)
            for n in range(2):
                into[pl.ds(r * 128, 128), pl.ds(n * half, half)] = contract(
                    lambda cols: right[0, mine, cols],
                    lambda cols: right[0, pl.ds(n * half, half), cols],
                    0, features, zero,
                )
        if into is self_out:
            self_copy.start()

    part_copies = [
        remote(
            part_out.at[pl.ds(start, count)], part_in.at[pl.ds(start, count)],
            part_send.at[g], part_recv.at[g], there(blk, y_other),
        )
        for g, (start, count) in enumerate(groups[:final])
    ]
    for n in range(2):
        cols = (slice(None), pl.ds(n * half, half))
        part_copies.append(
            remote(last_out.at[cols], last_in.at[cols], part_send.at[final + n], part_recv.at[final + n], there(blk, y_other))
        )

    def res_copy(g, slot, side):
        start, count = groups[g]
        return remote(
            staged.at[pl.ds(start, count)],
            tiles.at[slot, pl.ds(start % half, count), half_of(side)],
            res_send.at[g], res_recv.at[slot - 1, side, g], there(whose, start // half),
        )

    def last_res_copy(slot):
        start, count = groups[final]
        return remote(
            last_staged, tiles.at[slot, pl.ds(start % half, count), :],
            res_send.at[final], res_recv.at[slot - 1, 0, final], there(whose, start // half),
        )

    holds_last = y == groups[final][0] // half

    def wait_results(slot):
        for g, (start, _) in enumerate(groups):
            @pl.when(y == start // half)
            def _():
                if g == final:
                    last_res_copy(slot).wait_recv()
                else:
                    for side in range(2):
                        res_copy(g, slot, side).wait_recv()

    def turn_copy(n):
        cols = pl.ds(n * TURN, TURN)
        return remote(turned.at[:, cols], tiles.at[2, :, cols], turn_send.at[n], turn_recv.at[n], there(chip, y))

    def finish(g):
        start, count = groups[g]
        end = start + count
        here = pl.ds(start, count)
        for copy in part_copies[g : g + 1] if g < final else part_copies[final:]:
            copy.wait_recv()
        if g < final:
            summed = (part_keep[here, :] + part_in[here, :]) * scale
            part_keep[here, :] = summed
            staged[here, :] = summed.astype(jnp.bfloat16)

            @pl.when(near)
            def _():
                res_copy(g, made, y).start()
        else:
            @pl.when(holds_last)
            def _():
                last_staged[...] = ((last_out[...] + last_in[...]) * scale).astype(jnp.bfloat16)
                last_res_copy(made).start()

            part_keep[here, :] = (last_out[:, half_of(y)] + last_in[:, half_of(y)]) * scale
        if end % TURN == 0:
            block = part_keep[end - TURN : end, :].T.astype(jnp.bfloat16)

            @pl.when(borrows)
            def _():
                turned[:, end - TURN : end] = block
                turn_copy(end // TURN - 1).start()

            @pl.when(jnp.logical_not(borrows))
            def _():
                tiles[made, :, end - TURN : end] = block

    def influence_of(targets, slot):
        return lax.dot_general(targets[...], tiles[slot], NT, preferred_element_type=jnp.float32)

    def near_influence():
        infl[...] = influence_of(targ_own, 0) + influence_of(targ_chip, 1)

    targ_to_chip.wait_recv()

    @pl.when(borrows)
    def _():
        targ_lent.start()
        right_copy.wait_recv()

    load_targ.wait()
    pl.semaphore_wait(diag_sem, 1)
    at = 0
    for g, (start, count) in enumerate(groups):
        here = pl.ds(start, count)
        if g == final:
            @pl.when(lead)
            def _():
                wait_results(1)
                near_influence()
        for piece, (_, _, first, width) in enumerate(chunks[g]):
            if g == final and piece == 1:
                @pl.when(lead)
                def _():
                    for early in range(final - 1):
                        res_copy(early, made, y).start()

            left_copy(at, left_send, across + 1).wait_recv()
            at += 1
            if g == final:
                for n in range(2):
                    cols = pl.ds(n * half, half)
                    last_out[:, cols] = contract(
                        lambda k: left[here, k],
                        lambda k: right[right_at, cols, k],
                        first, width,
                        jnp.zeros((count, half), jnp.float32) if piece == 0 else last_out[:, cols],
                    )
                    if piece == len(chunks[g]) - 1:
                        part_copies[g + n].start()
                continue
            for into, side in ((part_out, y_other), (part_keep, y)):
                into[here, :] = contract(
                    lambda k: left[here, k],
                    lambda k: right[right_at, half_of(side), k],
                    first, width, jnp.zeros((count, half), jnp.float32),
                )
                if into is part_out:
                    part_copies[g].start()
        if g >= 1:
            finish(g - 1)
        if g == 0:
            self_copy.wait_recv()
            tiles[0] = ((self_keep[...] + self_in[...]) * scale).astype(jnp.bfloat16)

    @pl.when(lead)
    def _():
        res_copy(final - 1, made, y).start()

    @pl.when(odd_lead)
    def _():
        targ_to_far.start()

    @pl.when(borrows)
    def _():
        targ_to_pass.wait_recv()
        targ_passed.start()

    finish(final)

    @pl.when(near)
    def _():
        near_influence()

    targ_to_far.wait_recv()

    @pl.when(streams)
    def _():
        wait_results(2)

    @pl.when(lends)
    def _():
        for n in range(rows // TURN):
            turn_copy(n).wait_recv()

    infl[...] += influence_of(targ_far, 2)

    for copy in part_copies:
        copy.wait_send()
    for g in range(final):
        res_copy(g, made, y).wait_send()

    @pl.when(holds_last)
    def _():
        last_res_copy(made).wait_send()

    self_copy.wait_send()
    targ_to_chip.wait_send()

    @pl.when(streams)
    def _():
        for at in range(len(flat)):
            left_copy(at, left_send, across + 1).wait_send()

    @pl.when(lead)
    def _():
        for at in range(len(flat)):
            left_copy(at, chip_send, chip).wait_send()
        targ_to_far.wait_send()

    @pl.when(borrows)
    def _():
        targ_lent.wait_send()
        targ_passed.wait_send()
        for n in range(rows // TURN):
            turn_copy(n).wait_send()

    @pl.when(odd_near)
    def _():
        targ_to_pass.wait_send()

    @pl.when(lends)
    def _():
        right_copy.wait_send()


def put_kernel(tiles, infl, tiles_hbm, infl_hbm, sems):
    puts = [pltpu.make_async_copy(infl, infl_hbm, sems.at[3])]
    puts += [pltpu.make_async_copy(tiles.at[slot], tiles_hbm.at[slot], sems.at[slot]) for slot in range(3)]
    for put in puts:
        put.start()
    for put in puts:
        put.wait()


def per_device(gradients, targets):
    rows, features = gradients.shape
    half, columns = rows // 2, targets.shape[1]
    count = sum(len(pieces) for pieces in chunk_list(features))
    last, groups = GROUPS[-1][1], len(GROUPS)
    bf16, f32 = jnp.bfloat16, jnp.float32
    dma, vmem = pltpu.SemaphoreType.DMA, pltpu.VMEM
    shapes = (jax.ShapeDtypeStruct((3, half, rows), bf16), jax.ShapeDtypeStruct((columns, half), f32))
    tiles, infl = pl.pallas_call(
        functools.partial(kernel, 1.0 / (2 * features) ** 0.5),
        out_shape=shapes,
        in_specs=[pl.BlockSpec(memory_space=pltpu.HBM)] * 2,
        out_specs=[pl.BlockSpec(memory_space=vmem)] * 2,
        scratch_shapes=[
            vmem((2, rows, features), bf16),
            vmem((rows, features), bf16),
            *[vmem((columns, rows), bf16)] * 4,
            *[vmem((half, rows), f32)] * 3,
            *[vmem((rows, half), f32)] * 3,
            vmem((rows, half), bf16),
            vmem((last, rows), f32), vmem((last, rows), f32), vmem((last, rows), bf16),
            vmem((half, rows), bf16),
            pltpu.SemaphoreType.REGULAR, pltpu.SemaphoreType.REGULAR,
            dma, dma, dma((count,)), dma((count,)), dma((count,)), dma,
            dma((4,)), dma((3,)), dma, dma,
            dma((groups + 1,)), dma((groups + 1,)), dma((groups,)), dma((2, 2, groups)),
            dma((rows // TURN,)), dma((rows // TURN,)),
        ],
        compiler_params=pltpu.CompilerParams(
            collective_id=0, has_side_effects=True, vmem_limit_bytes=48 * 2**20
        ),
    )(pltpu.with_memory_space_constraint(gradients, pltpu.HBM), pltpu.with_memory_space_constraint(targets.T, pltpu.HBM))
    tiles, infl = pl.pallas_call(
        put_kernel,
        out_shape=shapes,
        in_specs=[pl.BlockSpec(memory_space=vmem)] * 2,
        out_specs=[pl.BlockSpec(memory_space=pltpu.HBM)] * 2,
        scratch_shapes=[dma((4,))],
        compiler_params=pltpu.CompilerParams(vmem_limit_bytes=16 * 2**20),
    )(tiles, infl)
    return tiles, infl.T


def solution(mesh):
    placed = (P("blk", "tgt"), P("blk", None))
    return jax.shard_map(
        per_device,
        mesh=mesh,
        in_specs=placed,
        out_specs=(P(None, ("blk", "tgt"), None), P(("blk", "tgt"), None)),
        check_vma=False,
    )
```
